32 devices in a mesh: group: 2 (over x), ctx: 16 (over z, y, core).
Axes of the slice: x: 2, y: 2, z: 4, core: 2. Of those that a mesh axis runs over, the one named last changes fastest.
Arguments:
- queries: bfloat16 [256, 8, 8192], P(('group', 'ctx')), parts along dimension 0, may hold values from -40 to 40
- kv_cache: bfloat16 [32, 2, 512, 1024], P(('group', 'ctx')), parts along dimension 0, may hold values from -16 to 16
- page_counts: int32 [16], P('group'), parts along dimension 0, may hold values from 1 to 6, as said below
- doc_ids: int32 [16], P('group'), parts along dimension 0, may hold values from 0 to 7, each once
Outputs:
- attended: bfloat16 [256, 8, 8192], P(('group', 'ctx')), parts along dimension 0
The draws below stay inside these ranges and needn't reach their ends.
There are 2 independent parts, one for each index of `group`. The reference program is written for one: setup_inputs(seed, part) draws one part's arguments, and reference() takes and returns one part's arrays. A program takes and returns all parts, laid end to end along the dimension named above; each array names one. Nothing has to cross between parts.
Inputs may be any that keep to these rules, and one draw needn't show every extreme that they name: `page_counts`: the counts sum to 16; every document holds at least 1 pages, some document exactly 1, and some document exactly 6. `doc_ids`: every document is named by exactly one question block.
All inputs are finite; a program needn't handle non-finite values.
Results may differ from the reference program's by a relative error of at most 0.0031.
Values may be sent and summed in bfloat16 or wider, within the bound.
A program may use at most 128 MiB of HBM per device.

```python
import jax
import jax.numpy as jnp
from jax import lax

HEADS = 64
KV_HEADS = 8
HEAD_DIM = 128
DOCS = 8
QUERY_TOK = 128
PAGE_TOK = 512
PAGES_DEV = 1
PAGES = 16


def draw_queries(key, part):
    width = HEADS * HEAD_DIM
    base = jax.random.truncated_normal(jax.random.fold_in(key, 21), -4.0, 4.0, (QUERY_TOK, DOCS, width), jnp.float32) * 2.0
    return base.astype(jnp.bfloat16)


def draw_kv_cache(key, part):
    noise = jax.random.truncated_normal(jax.random.fold_in(key, 31), -4.0, 4.0, (PAGES, 2, PAGE_TOK, KV_HEADS * HEAD_DIM), jnp.float32)
    key_part = noise[:, 0]
    value_part = 4.0 * noise[:, 1]
    return jnp.stack([key_part, value_part], axis=1).astype(jnp.bfloat16)


def draw_page_counts(key, part):
    most_pages = 3 * PAGES // DOCS
    middle = DOCS - 2
    rest_pages = PAGES - most_pages - PAGES_DEV
    extra_pages = rest_pages - middle * PAGES_DEV
    share_base = extra_pages // middle
    leftover = extra_pages % middle
    shares = share_base + (jnp.arange(middle, dtype=jnp.int32) < leftover).astype(jnp.int32)
    pair_count = middle // 2
    spread = max(0, min(share_base, most_pages - PAGES_DEV - share_base - 1))
    delta = jax.random.randint(jax.random.fold_in(key, 43), (pair_count,), 0, spread + 1).astype(jnp.int32)
    moved = jnp.zeros((middle,), jnp.int32)
    moved = moved.at[0:2 * pair_count:2].add(delta)
    moved = moved.at[1:2 * pair_count:2].add(-delta)
    middle_counts = PAGES_DEV + shares + moved
    counts = jnp.concatenate([jnp.full((1,), most_pages, jnp.int32), jnp.full((1,), PAGES_DEV, jnp.int32), middle_counts])
    shuffle = jax.random.permutation(jax.random.fold_in(key, 42), DOCS)
    return counts[shuffle].astype(jnp.int32)


def setup_inputs(seed: int = 0, part: int = 0) -> dict:
    key_list = jax.random.split(jax.random.key(seed), 5)
    own_keys = jax.random.split(jax.random.fold_in(key_list[4], part), 5)
    return {
        "queries": draw_queries(jax.random.fold_in(jax.random.fold_in(key_list[4], part), 71), part),
        "kv_cache": draw_kv_cache(jax.random.fold_in(jax.random.fold_in(key_list[4], part), 71), part),
        "page_counts": draw_page_counts(jax.random.fold_in(jax.random.fold_in(key_list[4], part), 71), part),
        "doc_ids": jax.random.permutation(own_keys[3], DOCS).astype(jnp.int32),
    }


def page_partial(rows, page_kv):
    tokens = rows.shape[0]
    kv_heads = page_kv.shape[-1] // HEAD_DIM
    groups = rows.shape[-1] // (kv_heads * HEAD_DIM)
    grouped = rows.astype(jnp.float32).reshape(tokens, kv_heads, groups, HEAD_DIM)
    keys = page_kv[0].astype(jnp.float32).reshape(-1, kv_heads, HEAD_DIM)
    values = page_kv[1].astype(jnp.float32).reshape(-1, kv_heads, HEAD_DIM)
    scores = jnp.einsum("qhgd,khd->qhgk", grouped, keys, precision=lax.Precision.HIGHEST) * (HEAD_DIM ** -0.5)
    row_max = jnp.max(scores, axis=-1)
    expo = jnp.exp(scores - row_max[..., None])
    row_sum = jnp.sum(expo, axis=-1)
    weights = lax.optimization_barrier(expo.astype(jnp.bfloat16)).astype(jnp.float32)
    mixed = jnp.einsum("qhgk,khd->qhgd", weights, values, precision=lax.Precision.HIGHEST)
    return row_max.reshape(tokens, -1), row_sum.reshape(tokens, -1), mixed.reshape(tokens, -1)


def reference(queries, kv_cache, page_counts, doc_ids):
    doc_ends = jnp.cumsum(page_counts).astype(jnp.int32)
    block_order = jnp.arange(DOCS, dtype=jnp.int32)
    width = HEADS * HEAD_DIM

    def visit(carry, page):
        big_max, big_sum, big_out = carry
        page_doc = jnp.sum((page >= doc_ends).astype(jnp.int32))
        block = jnp.sum(jnp.where(doc_ids == page_doc, block_order, 0)).astype(jnp.int32)
        rows = lax.dynamic_index_in_dim(queries, block, 1, keepdims=False)
        page_kv = lax.dynamic_index_in_dim(kv_cache, page.astype(jnp.int32), 0, keepdims=False)
        row_max, row_sum, mixed = page_partial(rows, page_kv)
        old_max = lax.dynamic_index_in_dim(big_max, block, 0, keepdims=False)
        old_sum = lax.dynamic_index_in_dim(big_sum, block, 0, keepdims=False)
        old_out = lax.dynamic_index_in_dim(big_out, block, 0, keepdims=False)
        new_max = jnp.maximum(old_max, row_max)
        keep_old = jnp.exp(old_max - new_max)
        keep_new = jnp.exp(row_max - new_max)
        new_sum = keep_old * old_sum + keep_new * row_sum
        tokens = rows.shape[0]
        new_out = (keep_old[..., None] * old_out.reshape(tokens, HEADS, HEAD_DIM)
                   + keep_new[..., None] * mixed.reshape(tokens, HEADS, HEAD_DIM)).reshape(tokens, width)
        big_max = lax.dynamic_update_index_in_dim(big_max, new_max, block, 0)
        big_sum = lax.dynamic_update_index_in_dim(big_sum, new_sum, block, 0)
        big_out = lax.dynamic_update_index_in_dim(big_out, new_out, block, 0)
        return (big_max, big_sum, big_out), None

    start = (jnp.full((DOCS, QUERY_TOK, HEADS), -1e30, jnp.float32),
             jnp.zeros((DOCS, QUERY_TOK, HEADS), jnp.float32),
             jnp.zeros((DOCS, QUERY_TOK, width), jnp.float32))
    pages = jnp.arange(PAGES, dtype=jnp.int32)
    (big_max, big_sum, big_out), unused = lax.scan(visit, start, pages)
    normed = big_out.reshape(DOCS, QUERY_TOK, HEADS, HEAD_DIM) / big_sum[..., None]
    normed = jnp.transpose(normed.reshape(DOCS, QUERY_TOK, width), (1, 0, 2))
    return normed.astype(jnp.bfloat16)
```

```python
import functools

import jax
import jax.numpy as jnp
from jax import lax
from jax.experimental import pallas as pl
from jax.experimental.pallas import tpu as pltpu
from jax.sharding import PartitionSpec as P

HEAD_DIM = 128
CHUNKS = 4


def exchange_kernel(
    peers, q_hbm, kv_hbm, got_hbm, stats_hbm,
    q_buf, o_buf, s_buf, kv_buf,
    q_send, q_recv, o_send, o_recv, s_send, s_recv, own_sem, kv_sem,
):
    chunks, _, rows, wide = q_buf.shape
    me = lax.axis_index("ctx")
    tokens = peers * rows
    heads_chunk = wide // HEAD_DIM
    kv_heads = kv_buf.shape[2] // HEAD_DIM
    groups = chunks * heads_chunk // kv_heads

    kv_copy = pltpu.make_async_copy(kv_hbm.at[0], kv_buf, kv_sem)
    kv_copy.start()
    own_q = pltpu.make_async_copy(q_hbm.at[:, me], q_buf.at[:, me], own_sem.at[0])
    own_q.start()

    barrier = pltpu.get_barrier_semaphore()

    @pl.loop(1, peers)
    def _(k):
        pl.semaphore_signal(
            barrier, inc=1, device_id={"ctx": lax.rem(me + k, peers)},
            device_id_type=pl.DeviceIdType.MESH,
        )

    pl.semaphore_wait(barrier, peers - 1)

    def send(src, dst, send_sem, recv_sem):
        @pl.loop(1, peers)
        def _(k):
            peer = lax.rem(me + k, peers)
            pltpu.make_async_remote_copy(
                src_ref=src.at[peer], dst_ref=dst.at[me], send_sem=send_sem,
                recv_sem=recv_sem, device_id={"ctx": peer},
                device_id_type=pl.DeviceIdType.MESH,
            ).start()

    def drain(ref, sem):
        part = ref.at[pl.ds(0, peers - 1)]
        pltpu.make_async_copy(part, part, sem).wait()

    for c in range(chunks):
        send(q_hbm.at[c], q_buf.at[c], q_send.at[c], q_recv.at[c])

    s_buf[...] = jnp.zeros_like(s_buf)
    kv_copy.wait()
    own_q.wait()
    lane = lax.broadcasted_iota(jnp.int32, (tokens, 128), 1)
    for c in range(chunks):
        drain(q_buf.at[c], q_recv.at[c])

        def head(j, carry):
            lanes = pl.ds(pl.multiple_of(j * HEAD_DIM, HEAD_DIM), HEAD_DIM)
            h = c * heads_chunk + j
            kv_lanes = pl.ds(pl.multiple_of(h // groups * HEAD_DIM, HEAD_DIM), HEAD_DIM)
            q = q_buf[c, :, :, lanes].astype(jnp.float32).reshape(tokens, HEAD_DIM)
            s = lax.dot_general(
                q.astype(jnp.bfloat16), kv_buf[0, :, kv_lanes], (((1,), (1,)), ((), ())),
                preferred_element_type=jnp.float32,
            ) * HEAD_DIM ** (-0.5)
            top = jnp.max(s, axis=-1, keepdims=True)
            p = jnp.exp(s - top)
            total = jnp.sum(p, axis=-1, keepdims=True)
            o = jnp.dot(
                p.astype(jnp.bfloat16), kv_buf[1, :, kv_lanes],
                preferred_element_type=jnp.float32,
            ) / total
            o_buf[c, :, :, lanes] = o.reshape(peers, rows, HEAD_DIM).astype(jnp.bfloat16)
            old = s_buf[...].reshape(tokens, 128)
            new = jnp.where(lane == h, top, jnp.where(lane == h + 64, total, old))
            s_buf[...] = new.reshape(peers, rows, 128)
            return carry

        lax.fori_loop(0, heads_chunk, head, 0)
        send(o_buf.at[c], got_hbm.at[c], o_send.at[c], o_recv.at[c])
    send(s_buf, stats_hbm, s_send, s_recv)
    own_o = pltpu.make_async_copy(o_buf.at[:, me], got_hbm.at[:, me], own_sem.at[0])
    own_o.start()
    own_s = pltpu.make_async_copy(s_buf.at[me], stats_hbm.at[me], own_sem.at[1])
    own_s.start()
    for c in range(chunks):
        drain(q_buf.at[c], q_send.at[c])
        drain(o_buf.at[c], o_send.at[c])
        drain(o_buf.at[c], o_recv.at[c])
    drain(s_buf, s_send)
    drain(s_buf, s_recv)
    own_o.wait()
    own_s.wait()


def exchange(outgoing, kv_cache, peers):
    chunks, _, rows, wide = outgoing.shape
    any_spec = pl.BlockSpec(memory_space=pl.ANY)
    dma = pltpu.SemaphoreType.DMA
    return pl.pallas_call(
        functools.partial(exchange_kernel, peers),
        out_shape=(
            jax.ShapeDtypeStruct(outgoing.shape, jnp.bfloat16),
            jax.ShapeDtypeStruct((peers, rows, 128), jnp.float32),
        ),
        in_specs=[any_spec, any_spec],
        out_specs=(any_spec, any_spec),
        scratch_shapes=[
            pltpu.VMEM(outgoing.shape, jnp.bfloat16),
            pltpu.VMEM(outgoing.shape, jnp.bfloat16),
            pltpu.VMEM((peers, rows, 128), jnp.float32),
            pltpu.VMEM(kv_cache.shape[1:], jnp.bfloat16),
            dma((chunks,)), dma((chunks,)), dma((chunks,)), dma((chunks,)),
            dma(()), dma(()), dma((2,)), dma(()),
        ],
        compiler_params=pltpu.CompilerParams(collective_id=0, has_side_effects=True),
    )(outgoing, kv_cache)


def combine_kernel(heads, fresh, last, got_ref, stats_ref, out_ref, w_buf, top_buf, run_buf):
    peers, rows, wide = run_buf.shape
    step = pl.program_id(0)

    @pl.when(step == 0)
    def _():
        def forward(n, top):
            mine = stats_ref[n]
            top = jnp.where(fresh[n] == 1, mine, jnp.maximum(top, mine))
            top_buf[n] = top
            return top

        def backward(i, top):
            n = peers - 1 - i
            top = jnp.where(fresh[n + 1] == 1, top_buf[n], top)
            top_buf[n] = top
            return top

        def weigh(n, total):
            mine = stats_ref[n]
            w = jnp.exp(mine - top_buf[n]) * pltpu.roll(mine, 128 - 64, 1)
            w_buf[n] = w
            total = jnp.where(fresh[n] == 1, w, total + w)
            top_buf[n] = total
            return total

        def norm(i, total):
            n = peers - 1 - i
            total = jnp.where(fresh[n + 1] == 1, top_buf[n], total)
            w_buf[n] = w_buf[n] / total
            return total

        zero = jnp.zeros(stats_ref.shape[1:], jnp.float32)
        lax.fori_loop(0, peers, forward, zero)
        lax.fori_loop(0, peers, backward, zero)
        lax.fori_loop(0, peers, weigh, zero)
        lax.fori_loop(0, peers, norm, zero)

    count = wide // HEAD_DIM

    def visit(n, acc):
        w = pltpu.roll(w_buf[n], lax.rem(128 - step * count, 128), 1)
        w = jnp.concatenate(
            [jnp.broadcast_to(w[:, i:i + 1], (rows, HEAD_DIM)) for i in range(count)], axis=1
        )
        mine = w * got_ref[0, n].astype(jnp.float32)
        acc = jnp.where(fresh[n] == 1, mine, acc + mine)
        run_buf[n] = acc
        return acc

    lax.fori_loop(0, peers, visit, jnp.zeros((rows, wide), jnp.float32), unroll=4)
    blocks = out_ref.shape[1]
    picked = jnp.stack([run_buf[last[c]] for c in range(blocks)], axis=0)
    out_ref[...] = jnp.swapaxes(picked, 0, 1).astype(jnp.bfloat16)


def combine(got, stats, fresh, last, heads):
    chunks, peers, rows, wide_all = got.shape
    wide = min(wide_all, 1024)
    per = wide_all // wide
    blocks = last.shape[0]
    width = chunks * wide_all
    return pl.pallas_call(
        functools.partial(combine_kernel, heads),
        out_shape=jax.ShapeDtypeStruct((rows, blocks, width), jnp.bfloat16),
        grid_spec=pltpu.PrefetchScalarGridSpec(
            num_scalar_prefetch=2,
            grid=(width // wide,),
            in_specs=[
                pl.BlockSpec((1, peers, rows, wide), lambda i, f, l: (i // per, 0, 0, i % per)),
                pl.BlockSpec((peers, rows, 128), lambda i, f, l: (0, 0, 0)),
            ],
            out_specs=pl.BlockSpec((rows, blocks, wide), lambda i, f, l: (0, 0, i)),
            scratch_shapes=[
                pltpu.VMEM((peers, rows, 128), jnp.float32),
                pltpu.VMEM((peers, rows, 128), jnp.float32),
                pltpu.VMEM((peers, rows, wide), jnp.float32),
            ],
        ),
    )(fresh, last, got, stats)


def body(queries, kv_cache, page_counts, doc_ids):
    peers = lax.axis_size("ctx")
    rows, blocks, width = queries.shape
    heads = width // HEAD_DIM
    assert kv_cache.shape[0] == 1 and heads == 64
    doc_ends = jnp.cumsum(page_counts)
    pages = jnp.arange(peers, dtype=jnp.int32)
    page_docs = jnp.sum((pages[:, None] >= doc_ends).astype(jnp.int32), axis=-1)
    block_order = jnp.arange(blocks, dtype=jnp.int32)
    page_blocks = jnp.sum(jnp.where(doc_ids[None, :] == page_docs[:, None], block_order, 0), axis=-1)
    edge = (page_docs[1:] != page_docs[:-1]).astype(jnp.int32)
    one = jnp.ones((1,), jnp.int32)
    fresh = jnp.concatenate([one, edge, one])
    last = jnp.sum(
        jnp.where(doc_ids[:, None] == block_order[None, :], doc_ends[None, :], 0), axis=-1
    ) - 1

    outgoing = jnp.take(queries, page_blocks, axis=1)
    outgoing = outgoing.reshape(rows, peers, CHUNKS, width // CHUNKS).transpose(2, 1, 0, 3)
    got, stats = exchange(outgoing, kv_cache, peers)
    return combine(got, stats, fresh, last.astype(jnp.int32), heads)


def solution(mesh):
    placed = (
        P(("group", "ctx"), None, None),
        P(("group", "ctx"), None, None, None),
        P("group"),
        P("group"),
    )
    return jax.shard_map(
        body, mesh=mesh, in_specs=placed, out_specs=P(("group", "ctx"), None, None), check_vma=False
    )
```

```python
import functools

import jax
import jax.numpy as jnp
from jax import lax
from jax.experimental import pallas as pl
from jax.experimental.pallas import tpu as pltpu
from jax.sharding import PartitionSpec as P

HEAD_DIM = 128
CHUNKS = 4


def attend_kernel(
    peers, counts, doc_ids, q_hbm, kv_hbm, out_hbm,
    raw_buf, doc_buf, send_buf, q_buf, o_buf, got_buf, s_buf, stats_buf, w_buf, top_buf,
    run_buf, out_buf, kv_buf, ends, page_doc, page_block, fresh,
    raw_sem, q_send, q_recv, o_send, o_recv, s_send, s_recv, own_q_sem, own_o_sem, own_s_sem,
    kv_sem, out_sem,
):
    chunks, _, rows, wide = q_buf.shape
    blocks = counts.shape[0]
    me = lax.axis_index("ctx")
    tokens = peers * rows
    heads_chunk = wide // HEAD_DIM
    kv_heads = kv_buf.shape[2] // HEAD_DIM
    groups = chunks * heads_chunk // kv_heads
    mesh_id = pl.DeviceIdType.MESH

    barrier = pltpu.get_barrier_semaphore()

    @pl.loop(1, peers)
    def _(k):
        pl.semaphore_signal(
            barrier, inc=1, device_id={"ctx": lax.rem(me + k, peers)}, device_id_type=mesh_id
        )

    def columns(c):
        return pl.ds(c * wide, wide)

    raw_copies = [
        pltpu.make_async_copy(q_hbm.at[:, :, columns(c)], raw_buf.at[c], raw_sem.at[c])
        for c in range(chunks)
    ]
    for copy in raw_copies:
        copy.start()
    kv_copy = pltpu.make_async_copy(kv_hbm.at[0], kv_buf, kv_sem)
    kv_copy.start()

    end = 0
    for j in range(blocks):
        end = end + counts[j]
        ends[j] = end

    def locate(n, before):
        doc = 0
        for j in range(blocks):
            doc = doc + (n >= ends[j]).astype(jnp.int32)
        block = 0
        for j in range(1, blocks):
            block = block + jnp.where(doc_ids[j] == doc, j, 0)
        page_doc[n] = doc
        page_block[n] = block
        fresh[n] = (doc != before).astype(jnp.int32)
        return doc

    lax.fori_loop(0, peers, locate, jnp.int32(-1))
    fresh[peers] = 1

    def send(src, dst, send_sem, recv_sem):
        @pl.loop(1, peers)
        def _(k):
            peer = lax.rem(me + k, peers)
            pltpu.make_async_remote_copy(
                src_ref=src.at[peer], dst_ref=dst.at[me], send_sem=send_sem,
                recv_sem=recv_sem, device_id={"ctx": peer}, device_id_type=mesh_id,
            ).start()

    def drain(ref, sem):
        part = ref.at[pl.ds(0, peers - 1)]
        pltpu.make_async_copy(part, part, sem).wait()

    own_q, own_o = [], []
    for c in range(chunks):
        raw_copies[c].wait()
        raw = raw_buf[c].astype(jnp.float32)
        doc_buf[c] = jnp.swapaxes(raw, 0, 1).astype(jnp.bfloat16)

        @pl.loop(0, peers)
        def _(n):
            send_buf[c, n] = doc_buf[c, page_block[n]]

        if c == 0:
            pl.semaphore_wait(barrier, peers - 1)
        send(send_buf.at[c], q_buf.at[c], q_send.at[c], q_recv.at[c])
        copy = pltpu.make_async_copy(send_buf.at[c, me], q_buf.at[c, me], own_q_sem.at[c])
        copy.start()
        own_q.append(copy)

    s_buf[...] = jnp.zeros_like(s_buf)
    kv_copy.wait()
    lane = lax.broadcasted_iota(jnp.int32, (tokens, 128), 1)
    own_s = pltpu.make_async_copy(s_buf.at[me], stats_buf.at[me], own_s_sem)
    for c in range(chunks):
        own_q[c].wait()
        drain(q_buf.at[c], q_recv.at[c])

        def head(j, carry):
            lanes = pl.ds(pl.multiple_of(j * HEAD_DIM, HEAD_DIM), HEAD_DIM)
            h = c * heads_chunk + j
            kv_lanes = pl.ds(pl.multiple_of(h // groups * HEAD_DIM, HEAD_DIM), HEAD_DIM)
            q = q_buf[c, :, :, lanes].astype(jnp.float32).reshape(tokens, HEAD_DIM)
            s = lax.dot_general(
                q.astype(jnp.bfloat16), kv_buf[0, :, kv_lanes], (((1,), (1,)), ((), ())),
                preferred_element_type=jnp.float32,
            ) * HEAD_DIM ** (-0.5)
            top = jnp.max(s, axis=-1, keepdims=True)
            p = jnp.exp(s - top)
            total = jnp.sum(p, axis=-1, keepdims=True)
            o = jnp.dot(
                p.astype(jnp.bfloat16), kv_buf[1, :, kv_lanes],
                preferred_element_type=jnp.float32,
            ) / total
            o_buf[c, :, :, lanes] = o.reshape(peers, rows, HEAD_DIM).astype(jnp.bfloat16)
            old = s_buf[...].reshape(tokens, 128)
            new = jnp.where(lane == h, top, jnp.where(lane == h + 64, total, old))
            s_buf[...] = new.reshape(peers, rows, 128)
            return carry

        lax.fori_loop(0, heads_chunk, head, 0)
        if c == chunks - 1:
            send(s_buf, stats_buf, s_send, s_recv)
            own_s.start()
        send(o_buf.at[c], got_buf.at[c], o_send.at[c], o_recv.at[c])
        copy = pltpu.make_async_copy(o_buf.at[c, me], got_buf.at[c, me], own_o_sem.at[c])
        copy.start()
        own_o.append(copy)

    own_s.wait()
    drain(stats_buf, s_recv)

    def forward(n, top):
        mine = stats_buf[n]
        top = jnp.where(fresh[n] == 1, mine, jnp.maximum(top, mine))
        top_buf[n] = top
        return top

    def backward(i, top):
        n = peers - 1 - i
        top = jnp.where(fresh[n + 1] == 1, top_buf[n], top)
        top_buf[n] = top
        return top

    def weigh(n, total):
        mine = stats_buf[n]
        w = jnp.exp(mine - top_buf[n]) * pltpu.roll(mine, 128 - 64, 1)
        w_buf[n] = w
        total = jnp.where(fresh[n] == 1, w, total + w)
        top_buf[n] = total
        return total

    def norm(i, total):
        n = peers - 1 - i
        total = jnp.where(fresh[n + 1] == 1, top_buf[n], total)
        w_buf[n] = w_buf[n] / total
        return total

    zero = jnp.zeros((rows, 128), jnp.float32)
    lax.fori_loop(0, peers, forward, zero)
    lax.fori_loop(0, peers, backward, zero)
    lax.fori_loop(0, peers, weigh, zero)
    lax.fori_loop(0, peers, norm, zero)

    outs = []
    for c in range(chunks):
        own_o[c].wait()
        drain(got_buf.at[c], o_recv.at[c])

        def visit(n, acc):
            w = w_buf[n]
            w = jnp.concatenate(
                [
                    jnp.broadcast_to(w[:, h:h + 1], (rows, HEAD_DIM))
                    for h in range(c * heads_chunk, (c + 1) * heads_chunk)
                ],
                axis=1,
            )
            mine = w * got_buf[c, n].astype(jnp.float32)
            acc = jnp.where(fresh[n] == 1, mine, acc + mine)
            run_buf[n] = acc
            return acc

        lax.fori_loop(0, peers, visit, jnp.zeros((rows, wide), jnp.float32), unroll=2)
        picked = jnp.stack([run_buf[jnp.clip(ends[doc_ids[b]] - 1, 0, peers - 1)] for b in range(blocks)], axis=0)
        out_buf[c] = jnp.swapaxes(picked, 0, 1).astype(jnp.bfloat16)
        copy = pltpu.make_async_copy(out_buf.at[c], out_hbm.at[:, :, columns(c)], out_sem.at[c])
        copy.start()
        outs.append(copy)
    drain(s_buf, s_send)
    for c in range(chunks):
        drain(send_buf.at[c], q_send.at[c])
        drain(o_buf.at[c], o_send.at[c])
        outs[c].wait()


def body(queries, kv_cache, page_counts, doc_ids):
    peers = lax.axis_size("ctx")
    rows, blocks, width = queries.shape
    assert kv_cache.shape[0] == 1 and width == 64 * HEAD_DIM
    wide = width // CHUNKS
    any_spec = pl.BlockSpec(memory_space=pl.ANY)
    smem_spec = pl.BlockSpec(memory_space=pltpu.SMEM)
    dma = pltpu.SemaphoreType.DMA
    pieces = pltpu.VMEM((CHUNKS, peers, rows, wide), jnp.bfloat16)
    stats = pltpu.VMEM((peers, rows, 128), jnp.float32)
    return pl.pallas_call(
        functools.partial(attend_kernel, peers),
        out_shape=jax.ShapeDtypeStruct(queries.shape, jnp.bfloat16),
        in_specs=[smem_spec, smem_spec, any_spec, any_spec],
        out_specs=any_spec,
        scratch_shapes=[
            pltpu.VMEM((CHUNKS, rows, blocks, wide), jnp.bfloat16),
            pltpu.VMEM((CHUNKS, blocks, rows, wide), jnp.bfloat16),
            pieces, pieces, pieces, pieces,
            stats, stats, stats, stats,
            pltpu.VMEM((peers, rows, wide), jnp.float32),
            pltpu.VMEM((CHUNKS, rows, blocks, wide), jnp.bfloat16),
            pltpu.VMEM(kv_cache.shape[1:], jnp.bfloat16),
            pltpu.SMEM((blocks,), jnp.int32),
            pltpu.SMEM((peers,), jnp.int32),
            pltpu.SMEM((peers,), jnp.int32),
            pltpu.SMEM((peers + 1,), jnp.int32),
            dma((CHUNKS,)),
            dma((CHUNKS,)), dma((CHUNKS,)), dma((CHUNKS,)), dma((CHUNKS,)),
            dma(()), dma(()), dma((CHUNKS,)), dma((CHUNKS,)), dma(()),
            dma(()), dma((CHUNKS,)),
        ],
        compiler_params=pltpu.CompilerParams(collective_id=0, has_side_effects=True),
    )(page_counts, doc_ids, queries, kv_cache)


def solution(mesh):
    placed = (
        P(("group", "ctx"), None, None),
        P(("group", "ctx"), None, None, None),
        P("group"),
        P("group"),
    )
    return jax.shard_map(
        body, mesh=mesh, in_specs=placed, out_specs=P(("group", "ctx"), None, None), check_vma=False
    )
```

```python
import functools

import jax
import jax.numpy as jnp
from jax import lax
from jax.experimental import pallas as pl
from jax.experimental.pallas import tpu as pltpu
from jax.sharding import PartitionSpec as P

HEAD_DIM = 128
CHUNKS = 8


def attend_kernel(
    peers, counts, doc_ids, q_hbm, kv_hbm, out_hbm,
    raw_buf, doc_buf, send_buf, q_buf, o_buf, got_buf, s_buf, stats_buf, w_buf, top_buf,
    run_buf, out_buf, kv_buf, ends, page_doc, page_block, fresh,
    raw_sem, q_send, q_recv, o_send, o_recv, s_send, s_recv, own_q_sem, own_o_sem, own_s_sem,
    kv_sem, out_sem,
):
    chunks, _, rows, wide = q_buf.shape
    blocks = counts.shape[0]
    me = lax.axis_index("ctx")
    tokens = peers * rows
    heads_chunk = wide // HEAD_DIM
    kv_heads = kv_buf.shape[2] // HEAD_DIM
    groups = chunks * heads_chunk // kv_heads
    mesh_id = pl.DeviceIdType.MESH

    barrier = pltpu.get_barrier_semaphore()

    @pl.loop(1, peers)
    def _(k):
        pl.semaphore_signal(
            barrier, inc=1, device_id={"ctx": lax.rem(me + k, peers)}, device_id_type=mesh_id
        )

    def columns(c):
        return pl.ds(c * wide, wide)

    raw_copies = [
        pltpu.make_async_copy(q_hbm.at[:, :, columns(c)], raw_buf.at[c], raw_sem.at[c])
        for c in range(chunks)
    ]
    for copy in raw_copies:
        copy.start()
    kv_copy = pltpu.make_async_copy(kv_hbm.at[0], kv_buf, kv_sem)
    kv_copy.start()

    end = 0
    for j in range(blocks):
        end = end + counts[j]
        ends[j] = end

    def locate(n, before):
        doc = 0
        for j in range(blocks):
            doc = doc + (n >= ends[j]).astype(jnp.int32)
        block = 0
        for j in range(1, blocks):
            block = block + jnp.where(doc_ids[j] == doc, j, 0)
        page_doc[n] = doc
        page_block[n] = block
        fresh[n] = (doc != before).astype(jnp.int32)
        return doc

    lax.fori_loop(0, peers, locate, jnp.int32(-1))
    fresh[peers] = 1

    def send(src, dst, send_sem, recv_sem):
        @pl.loop(1, peers)
        def _(k):
            peer = lax.rem(me + k, peers)
            pltpu.make_async_remote_copy(
                src_ref=src.at[peer], dst_ref=dst.at[me], send_sem=send_sem,
                recv_sem=recv_sem, device_id={"ctx": peer}, device_id_type=mesh_id,
            ).start()

    def drain(ref, sem):
        part = ref.at[pl.ds(0, peers - 1)]
        pltpu.make_async_copy(part, part, sem).wait()

    own_q, own_o = [], []
    for c in range(chunks):
        raw_copies[c].wait()
        raw = raw_buf[c].astype(jnp.float32)
        doc_buf[c] = jnp.swapaxes(raw, 0, 1).astype(jnp.bfloat16)

        @pl.loop(0, peers)
        def _(n):
            send_buf[c, n] = doc_buf[c, page_block[n]]

        if c == 0:
            pl.semaphore_wait(barrier, peers - 1)
        send(send_buf.at[c], q_buf.at[c], q_send.at[c], q_recv.at[c])
        copy = pltpu.make_async_copy(send_buf.at[c, me], q_buf.at[c, me], own_q_sem.at[c])
        copy.start()
        own_q.append(copy)

    s_buf[...] = jnp.zeros_like(s_buf)
    kv_copy.wait()
    lane = lax.broadcasted_iota(jnp.int32, (tokens, 128), 1)
    own_s = pltpu.make_async_copy(s_buf.at[me], stats_buf.at[me], own_s_sem)
    for c in range(chunks):
        own_q[c].wait()
        drain(q_buf.at[c], q_recv.at[c])

        def head(j, carry):
            lanes = pl.ds(pl.multiple_of(j * HEAD_DIM, HEAD_DIM), HEAD_DIM)
            h = c * heads_chunk + j
            kv_lanes = pl.ds(pl.multiple_of(h // groups * HEAD_DIM, HEAD_DIM), HEAD_DIM)
            q = q_buf[c, :, :, lanes].astype(jnp.float32).reshape(tokens, HEAD_DIM)
            s = lax.dot_general(
                q.astype(jnp.bfloat16), kv_buf[0, :, kv_lanes], (((1,), (1,)), ((), ())),
                preferred_element_type=jnp.float32,
            ) * HEAD_DIM ** (-0.5)
            top = jnp.max(s, axis=-1, keepdims=True)
            p = jnp.exp(s - top)
            total = jnp.sum(p, axis=-1, keepdims=True)
            o = jnp.dot(
                p.astype(jnp.bfloat16), kv_buf[1, :, kv_lanes],
                preferred_element_type=jnp.float32,
            ) / total
            o_buf[c, :, :, lanes] = o.reshape(peers, rows, HEAD_DIM).astype(jnp.bfloat16)
            old = s_buf[...].reshape(tokens, 128)
            new = jnp.where(lane == h, top, jnp.where(lane == h + 64, total, old))
            s_buf[...] = new.reshape(peers, rows, 128)
            return carry

        lax.fori_loop(0, heads_chunk, head, 0)
        if c == chunks - 1:
            send(s_buf, stats_buf, s_send, s_recv)
            own_s.start()
        send(o_buf.at[c], got_buf.at[c], o_send.at[c], o_recv.at[c])
        copy = pltpu.make_async_copy(o_buf.at[c, me], got_buf.at[c, me], own_o_sem.at[c])
        copy.start()
        own_o.append(copy)

    own_s.wait()
    drain(stats_buf, s_recv)

    def forward(n, top):
        mine = stats_buf[n]
        top = jnp.where(fresh[n] == 1, mine, jnp.maximum(top, mine))
        top_buf[n] = top
        return top

    def backward(i, top):
        n = peers - 1 - i
        top = jnp.where(fresh[n + 1] == 1, top_buf[n], top)
        top_buf[n] = top
        return top

    def weigh(n, total):
        mine = stats_buf[n]
        w = jnp.exp(mine - top_buf[n]) * pltpu.roll(mine, 128 - 64, 1)
        w_buf[n] = w
        total = jnp.where(fresh[n] == 1, w, total + w)
        top_buf[n] = total
        return total

    def norm(i, total):
        n = peers - 1 - i
        total = jnp.where(fresh[n + 1] == 1, top_buf[n], total)
        w_buf[n] = w_buf[n] / total
        return total

    zero = jnp.zeros((rows, 128), jnp.float32)
    lax.fori_loop(0, peers, forward, zero)
    lax.fori_loop(0, peers, backward, zero)
    lax.fori_loop(0, peers, weigh, zero)
    lax.fori_loop(0, peers, norm, zero)

    outs = []
    for c in range(chunks):
        own_o[c].wait()
        drain(got_buf.at[c], o_recv.at[c])

        def visit(n, acc):
            w = w_buf[n]
            w = jnp.concatenate(
                [
                    jnp.broadcast_to(w[:, h:h + 1], (rows, HEAD_DIM))
                    for h in range(c * heads_chunk, (c + 1) * heads_chunk)
                ],
                axis=1,
            )
            mine = w * got_buf[c, n].astype(jnp.float32)
            acc = jnp.where(fresh[n] == 1, mine, acc + mine)
            run_buf[n] = acc
            return acc

        lax.fori_loop(0, peers, visit, jnp.zeros((rows, wide), jnp.float32), unroll=2)
        picked = jnp.stack([run_buf[jnp.clip(ends[doc_ids[b]] - 1, 0, peers - 1)] for b in range(blocks)], axis=0)
        out_buf[c] = jnp.swapaxes(picked, 0, 1).astype(jnp.bfloat16)
        copy = pltpu.make_async_copy(out_buf.at[c], out_hbm.at[:, :, columns(c)], out_sem.at[c])
        copy.start()
        outs.append(copy)
    drain(s_buf, s_send)
    for c in range(chunks):
        drain(send_buf.at[c], q_send.at[c])
        drain(o_buf.at[c], o_send.at[c])
        outs[c].wait()


def body(queries, kv_cache, page_counts, doc_ids):
    peers = lax.axis_size("ctx")
    rows, blocks, width = queries.shape
    assert kv_cache.shape[0] == 1 and width == 64 * HEAD_DIM
    wide = width // CHUNKS
    any_spec = pl.BlockSpec(memory_space=pl.ANY)
    smem_spec = pl.BlockSpec(memory_space=pltpu.SMEM)
    dma = pltpu.SemaphoreType.DMA
    pieces = pltpu.VMEM((CHUNKS, peers, rows, wide), jnp.bfloat16)
    stats = pltpu.VMEM((peers, rows, 128), jnp.float32)
    return pl.pallas_call(
        functools.partial(attend_kernel, peers),
        out_shape=jax.ShapeDtypeStruct(queries.shape, jnp.bfloat16),
        in_specs=[smem_spec, smem_spec, any_spec, any_spec],
        out_specs=any_spec,
        scratch_shapes=[
            pltpu.VMEM((CHUNKS, rows, blocks, wide), jnp.bfloat16),
            pltpu.VMEM((CHUNKS, blocks, rows, wide), jnp.bfloat16),
            pieces, pieces, pieces, pieces,
            stats, stats, stats, stats,
            pltpu.VMEM((peers, rows, wide), jnp.float32),
            pltpu.VMEM((CHUNKS, rows, blocks, wide), jnp.bfloat16),
            pltpu.VMEM(kv_cache.shape[1:], jnp.bfloat16),
            pltpu.SMEM((blocks,), jnp.int32),
            pltpu.SMEM((peers,), jnp.int32),
            pltpu.SMEM((peers,), jnp.int32),
            pltpu.SMEM((peers + 1,), jnp.int32),
            dma((CHUNKS,)),
            dma((CHUNKS,)), dma((CHUNKS,)), dma((CHUNKS,)), dma((CHUNKS,)),
            dma(()), dma(()), dma((CHUNKS,)), dma((CHUNKS,)), dma(()),
            dma(()), dma((CHUNKS,)),
        ],
        compiler_params=pltpu.CompilerParams(collective_id=0, has_side_effects=True),
    )(page_counts, doc_ids, queries, kv_cache)


def solution(mesh):
    placed = (
        P(("group", "ctx"), None, None),
        P(("group", "ctx"), None, None, None),
        P("group"),
        P("group"),
    )
    return jax.shard_map(
        body, mesh=mesh, in_specs=placed, out_specs=P(("group", "ctx"), None, None), check_vma=False
    )
```

```python
import functools

import jax
import jax.numpy as jnp
from jax import lax
from jax.experimental import pallas as pl
from jax.experimental.pallas import tpu as pltpu
from jax.sharding import PartitionSpec as P

HEAD_DIM = 128
CHUNKS = 4
Q_CHUNKS = 4


def attend_kernel(
    peers, counts, doc_ids, q_hbm, kv_hbm, out_ref,
    raw_buf, doc_buf, send_buf, q_buf, o_buf, got_buf, s_buf, stats_buf, w_buf, top_buf,
    run_buf, wide_buf, kv_buf, ends, page_doc, page_block, fresh,
    raw_sem, q_send, q_recv, o_send, o_recv, s_send, s_recv, own_q_sem, own_o_sem, own_s_sem,
    kv_sem,
):
    chunks, _, rows, wide = o_buf.shape
    q_chunks, _, _, q_wide = q_buf.shape
    blocks = counts.shape[0]
    me = lax.axis_index("ctx")
    tokens = peers * rows
    heads_chunk = wide // HEAD_DIM
    kv_heads = kv_buf.shape[2] // HEAD_DIM
    groups = chunks * heads_chunk // kv_heads
    mesh_id = pl.DeviceIdType.MESH

    barrier = pltpu.get_barrier_semaphore()

    @pl.loop(1, peers)
    def _(k):
        pl.semaphore_signal(
            barrier, inc=1, device_id={"ctx": lax.rem(me + k, peers)}, device_id_type=mesh_id
        )

    raw_copies = [
        pltpu.make_async_copy(
            q_hbm.at[:, :, pl.ds(c * q_wide, q_wide)], raw_buf.at[c], raw_sem.at[c]
        )
        for c in range(q_chunks)
    ]
    for copy in raw_copies:
        copy.start()
    kv_copy = pltpu.make_async_copy(kv_hbm.at[0], kv_buf, kv_sem)
    kv_copy.start()

    end = 0
    for j in range(blocks):
        end = end + counts[j]
        ends[j] = end

    def locate(n, before):
        doc = 0
        for j in range(blocks):
            doc = doc + (n >= ends[j]).astype(jnp.int32)
        block = 0
        for j in range(1, blocks):
            block = block + jnp.where(doc_ids[j] == doc, j, 0)
        page_doc[n] = doc
        page_block[n] = block
        fresh[n] = (doc != before).astype(jnp.int32)
        return doc

    lax.fori_loop(0, peers, locate, jnp.int32(-1))
    fresh[peers] = 1

    def send(src, dst, send_sem, recv_sem):
        @pl.loop(1, peers)
        def _(k):
            peer = lax.rem(me + k, peers)
            pltpu.make_async_remote_copy(
                src_ref=src.at[peer], dst_ref=dst.at[me], send_sem=send_sem,
                recv_sem=recv_sem, device_id={"ctx": peer}, device_id_type=mesh_id,
            ).start()

    def drain(ref, sem):
        part = ref.at[pl.ds(0, peers - 1)]
        pltpu.make_async_copy(part, part, sem).wait()

    own_q, own_o = [], []
    for c in range(q_chunks):
        raw_copies[c].wait()
        raw = raw_buf[c].astype(jnp.float32)
        doc_buf[c] = jnp.swapaxes(raw, 0, 1).astype(jnp.bfloat16)

        @pl.loop(0, peers)
        def _(n):
            send_buf[c, n] = doc_buf[c, page_block[n]]

        if c == 0:
            pl.semaphore_wait(barrier, peers - 1)
        send(send_buf.at[c], q_buf.at[c], q_send.at[c], q_recv.at[c])
        copy = pltpu.make_async_copy(send_buf.at[c, me], q_buf.at[c, me], own_q_sem.at[c])
        copy.start()
        own_q.append(copy)

    s_buf[...] = jnp.zeros_like(s_buf)
    kv_copy.wait()
    lane = lax.broadcasted_iota(jnp.int32, (tokens, 128), 1)
    own_s = pltpu.make_async_copy(s_buf.at[me], stats_buf.at[me], own_s_sem)
    for c in range(chunks):
        piece, offset = divmod(c * wide, q_wide)
        if offset == 0:
            own_q[piece].wait()
            drain(q_buf.at[piece], q_recv.at[piece])

        def head(j, carry):
            lanes = pl.ds(pl.multiple_of(j * HEAD_DIM, HEAD_DIM), HEAD_DIM)
            h = c * heads_chunk + j
            kv_lanes = pl.ds(pl.multiple_of(h // groups * HEAD_DIM, HEAD_DIM), HEAD_DIM)
            q_lanes = pl.ds(pl.multiple_of(offset + j * HEAD_DIM, HEAD_DIM), HEAD_DIM)
            q = q_buf[piece, :, :, q_lanes].astype(jnp.float32).reshape(tokens, HEAD_DIM)
            s = lax.dot_general(
                q.astype(jnp.bfloat16), kv_buf[0, :, kv_lanes], (((1,), (1,)), ((), ())),
                preferred_element_type=jnp.float32,
            ) * HEAD_DIM ** (-0.5)
            top = jnp.max(s, axis=-1, keepdims=True)
            p = jnp.exp(s - top)
            total = jnp.sum(p, axis=-1, keepdims=True)
            o = jnp.dot(
                p.astype(jnp.bfloat16), kv_buf[1, :, kv_lanes],
                preferred_element_type=jnp.float32,
            ) / total
            o_buf[c, :, :, lanes] = o.reshape(peers, rows, HEAD_DIM).astype(jnp.bfloat16)
            old = s_buf[...].reshape(tokens, 128)
            new = jnp.where(lane == h, top, jnp.where(lane == h + 64, total, old))
            s_buf[...] = new.reshape(peers, rows, 128)
            return carry

        lax.fori_loop(0, heads_chunk, head, 0)
        if c == chunks - 1:
            send(s_buf, stats_buf, s_send, s_recv)
            own_s.start()
        send(o_buf.at[c], got_buf.at[c], o_send.at[c], o_recv.at[c])
        copy = pltpu.make_async_copy(o_buf.at[c, me], got_buf.at[c, me], own_o_sem.at[c])
        copy.start()
        own_o.append(copy)

    own_s.wait()
    drain(stats_buf, s_recv)

    def forward(n, top):
        mine = stats_buf[n]
        top = jnp.where(fresh[n] == 1, mine, jnp.maximum(top, mine))
        top_buf[n] = top
        return top

    def backward(i, top):
        n = peers - 1 - i
        top = jnp.where(fresh[n + 1] == 1, top_buf[n], top)
        top_buf[n] = top
        return top

    def weigh(n, total):
        mine = stats_buf[n]
        w = jnp.exp(mine - top_buf[n]) * pltpu.roll(mine, 128 - 64, 1)
        w_buf[n] = w
        total = jnp.where(fresh[n] == 1, w, total + w)
        top_buf[n] = total
        return total

    def norm(i, total):
        n = peers - 1 - i
        total = jnp.where(fresh[n + 1] == 1, top_buf[n], total)
        w_buf[n] = w_buf[n] / total
        return total

    zero = jnp.zeros((rows, 128), jnp.float32)
    lax.fori_loop(0, peers, forward, zero)
    lax.fori_loop(0, peers, backward, zero)
    lax.fori_loop(0, peers, weigh, zero)
    lax.fori_loop(0, peers, norm, zero)

    for c in range(chunks):

        @pl.loop(0, peers)
        def _(n):
            w = w_buf[n]
            for i in range(heads_chunk):
                h = c * heads_chunk + i
                wide_buf[n, :, i * HEAD_DIM:(i + 1) * HEAD_DIM] = jnp.broadcast_to(
                    w[:, h:h + 1], (rows, HEAD_DIM)
                )

        own_o[c].wait()
        drain(got_buf.at[c], o_recv.at[c])

        def visit(n, acc):
            mine = wide_buf[n] * got_buf[c, n].astype(jnp.float32)
            acc = jnp.where(fresh[n] == 1, mine, acc + mine)
            run_buf[n] = acc
            return acc

        lax.fori_loop(0, peers, visit, jnp.zeros((rows, wide), jnp.float32), unroll=2)
        picked = jnp.stack([run_buf[jnp.clip(ends[doc_ids[b]] - 1, 0, peers - 1)] for b in range(blocks)], axis=0)
        out_ref[:, :, c * wide:(c + 1) * wide] = jnp.swapaxes(picked, 0, 1).astype(jnp.bfloat16)
    drain(s_buf, s_send)
    for c in range(q_chunks):
        drain(send_buf.at[c], q_send.at[c])
    for c in range(chunks):
        drain(o_buf.at[c], o_send.at[c])


def body(queries, kv_cache, page_counts, doc_ids):
    peers = lax.axis_size("ctx")
    rows, blocks, width = queries.shape
    assert kv_cache.shape[0] == 1 and width == 64 * HEAD_DIM
    wide = width // CHUNKS
    q_wide = width // Q_CHUNKS
    hbm_spec = pl.BlockSpec(memory_space=pltpu.HBM)
    smem_spec = pl.BlockSpec(memory_space=pltpu.SMEM)
    dma = pltpu.SemaphoreType.DMA
    q_pieces = pltpu.VMEM((Q_CHUNKS, peers, rows, q_wide), jnp.bfloat16)
    pieces = pltpu.VMEM((CHUNKS, peers, rows, wide), jnp.bfloat16)
    stats = pltpu.VMEM((peers, rows, 128), jnp.float32)
    return pl.pallas_call(
        functools.partial(attend_kernel, peers),
        out_shape=jax.ShapeDtypeStruct(queries.shape, jnp.bfloat16),
        in_specs=[smem_spec, smem_spec, hbm_spec, hbm_spec],
        out_specs=pl.BlockSpec(memory_space=pltpu.VMEM),
        scratch_shapes=[
            pltpu.VMEM((Q_CHUNKS, rows, blocks, q_wide), jnp.bfloat16),
            pltpu.VMEM((Q_CHUNKS, blocks, rows, q_wide), jnp.bfloat16),
            q_pieces, q_pieces, pieces, pieces,
            stats, stats, stats, stats,
            pltpu.VMEM((peers, rows, wide), jnp.float32),
            pltpu.VMEM((peers, rows, wide), jnp.float32),
            pltpu.VMEM(kv_cache.shape[1:], jnp.bfloat16),
            pltpu.SMEM((blocks,), jnp.int32),
            pltpu.SMEM((peers,), jnp.int32),
            pltpu.SMEM((peers,), jnp.int32),
            pltpu.SMEM((peers + 1,), jnp.int32),
            dma((Q_CHUNKS,)),
            dma((Q_CHUNKS,)), dma((Q_CHUNKS,)), dma((CHUNKS,)), dma((CHUNKS,)),
            dma(()), dma(()), dma((Q_CHUNKS,)), dma((CHUNKS,)), dma(()),
            dma(()),
        ],
        compiler_params=pltpu.CompilerParams(collective_id=0, has_side_effects=True, vmem_limit_bytes=32 << 20),
    )(page_counts, doc_ids, queries, kv_cache)


def solution(mesh):
    placed = (
        P(("group", "ctx"), None, None),
        P(("group", "ctx"), None, None, None),
        P("group"),
        P("group"),
    )
    return jax.shard_map(
        body, mesh=mesh, in_specs=placed, out_specs=P(("group", "ctx"), None, None), check_vma=False
    )
```

```python
import functools

import jax
import jax.numpy as jnp
from jax import lax
from jax.experimental import pallas as pl
from jax.experimental.pallas import tpu as pltpu
from jax.sharding import PartitionSpec as P

HEAD_DIM = 128
CHUNKS = 4
Q_CHUNKS = 4


def attend_kernel(
    peers, counts, doc_ids, q_hbm, kv_hbm, out_hbm,
    raw_buf, doc_buf, send_buf, q_buf, o_buf, got_buf, s_buf, stats_buf, w_buf, top_buf,
    run_buf, wide_buf, out_buf, kv_buf, ends, page_doc, page_block, fresh,
    raw_sem, q_send, q_recv, o_send, o_recv, s_send, s_recv, own_q_sem, own_o_sem, own_s_sem,
    kv_sem, out_sem,
):
    chunks, _, rows, wide = o_buf.shape
    q_chunks, _, _, q_wide = q_buf.shape
    blocks = counts.shape[0]
    me = lax.axis_index("ctx")
    tokens = peers * rows
    heads_chunk = wide // HEAD_DIM
    kv_heads = kv_buf.shape[2] // HEAD_DIM
    groups = chunks * heads_chunk // kv_heads
    mesh_id = pl.DeviceIdType.MESH

    barrier = pltpu.get_barrier_semaphore()

    @pl.loop(1, peers)
    def _(k):
        pl.semaphore_signal(
            barrier, inc=1, device_id={"ctx": lax.rem(me + k, peers)}, device_id_type=mesh_id
        )

    raw_copies = [
        pltpu.make_async_copy(
            q_hbm.at[:, :, pl.ds(c * q_wide, q_wide)], raw_buf.at[c], raw_sem.at[c]
        )
        for c in range(q_chunks)
    ]
    for copy in raw_copies:
        copy.start()
    kv_copy = pltpu.make_async_copy(kv_hbm.at[0], kv_buf, kv_sem)
    kv_copy.start()

    end = 0
    for j in range(blocks):
        end = end + counts[j]
        ends[j] = end

    def locate(n, before):
        doc = 0
        for j in range(blocks):
            doc = doc + (n >= ends[j]).astype(jnp.int32)
        block = 0
        for j in range(1, blocks):
            block = block + jnp.where(doc_ids[j] == doc, j, 0)
        page_doc[n] = doc
        page_block[n] = block
        fresh[n] = (doc != before).astype(jnp.int32)
        return doc

    lax.fori_loop(0, peers, locate, jnp.int32(-1))
    fresh[peers] = 1

    def send(src, dst, send_sem, recv_sem):
        @pl.loop(1, peers)
        def _(k):
            peer = lax.rem(me + k, peers)
            pltpu.make_async_remote_copy(
                src_ref=src.at[peer], dst_ref=dst.at[me], send_sem=send_sem,
                recv_sem=recv_sem, device_id={"ctx": peer}, device_id_type=mesh_id,
            ).start()

    def drain(ref, sem):
        part = ref.at[pl.ds(0, peers - 1)]
        pltpu.make_async_copy(part, part, sem).wait()

    own_q, own_o = [], []
    for c in range(q_chunks):
        raw_copies[c].wait()
        raw = raw_buf[c].astype(jnp.float32)
        doc_buf[c] = jnp.swapaxes(raw, 0, 1).astype(jnp.bfloat16)

        @pl.loop(0, peers)
        def _(n):
            send_buf[c, n] = doc_buf[c, page_block[n]]

        if c == 0:
            pl.semaphore_wait(barrier, peers - 1)
        send(send_buf.at[c], q_buf.at[c], q_send.at[c], q_recv.at[c])
        copy = pltpu.make_async_copy(send_buf.at[c, me], q_buf.at[c, me], own_q_sem.at[c])
        copy.start()
        own_q.append(copy)

    s_buf[...] = jnp.zeros_like(s_buf)
    kv_copy.wait()
    lane = lax.broadcasted_iota(jnp.int32, (tokens, 128), 1)
    own_s = pltpu.make_async_copy(s_buf.at[me], stats_buf.at[me], own_s_sem)
    for c in range(chunks):
        piece, offset = divmod(c * wide, q_wide)
        if offset == 0:
            own_q[piece].wait()
            drain(q_buf.at[piece], q_recv.at[piece])

        def head(j, carry):
            lanes = pl.ds(pl.multiple_of(j * HEAD_DIM, HEAD_DIM), HEAD_DIM)
            h = c * heads_chunk + j
            kv_lanes = pl.ds(pl.multiple_of(h // groups * HEAD_DIM, HEAD_DIM), HEAD_DIM)
            q_lanes = pl.ds(pl.multiple_of(offset + j * HEAD_DIM, HEAD_DIM), HEAD_DIM)
            q = q_buf[piece, :, :, q_lanes].astype(jnp.float32).reshape(tokens, HEAD_DIM)
            s = lax.dot_general(
                q.astype(jnp.bfloat16), kv_buf[0, :, kv_lanes], (((1,), (1,)), ((), ())),
                preferred_element_type=jnp.float32,
            ) * HEAD_DIM ** (-0.5)
            top = jnp.max(s, axis=-1, keepdims=True)
            p = jnp.exp(s - top)
            total = jnp.sum(p, axis=-1, keepdims=True)
            o = jnp.dot(
                p.astype(jnp.bfloat16), kv_buf[1, :, kv_lanes],
                preferred_element_type=jnp.float32,
            ) / total
            o_buf[c, :, :, lanes] = o.reshape(peers, rows, HEAD_DIM).astype(jnp.bfloat16)
            old = s_buf[...].reshape(tokens, 128)
            new = jnp.where(lane == h, top, jnp.where(lane == h + 64, total, old))
            s_buf[...] = new.reshape(peers, rows, 128)
            return carry

        lax.fori_loop(0, heads_chunk, head, 0)
        if c == chunks - 1:
            send(s_buf, stats_buf, s_send, s_recv)
            own_s.start()
        for i in {0: [0], chunks - 1: range(1, chunks)}.get(c, []):
            send(o_buf.at[i], got_buf.at[i], o_send.at[i], o_recv.at[i])
        copy = pltpu.make_async_copy(o_buf.at[c, me], got_buf.at[c, me], own_o_sem.at[c])
        copy.start()
        own_o.append(copy)

    own_s.wait()
    drain(stats_buf, s_recv)

    def forward(n, top):
        mine = stats_buf[n]
        top = jnp.where(fresh[n] == 1, mine, jnp.maximum(top, mine))
        top_buf[n] = top
        return top

    def backward(i, top):
        n = peers - 1 - i
        top = jnp.where(fresh[n + 1] == 1, top_buf[n], top)
        top_buf[n] = top
        return top

    def weigh(n, total):
        mine = stats_buf[n]
        w = jnp.exp(mine - top_buf[n]) * pltpu.roll(mine, 128 - 64, 1)
        w_buf[n] = w
        total = jnp.where(fresh[n] == 1, w, total + w)
        top_buf[n] = total
        return total

    def norm(i, total):
        n = peers - 1 - i
        total = jnp.where(fresh[n + 1] == 1, top_buf[n], total)
        w_buf[n] = w_buf[n] / total
        return total

    zero = jnp.zeros((rows, 128), jnp.float32)
    lax.fori_loop(0, peers, forward, zero)
    lax.fori_loop(0, peers, backward, zero)
    lax.fori_loop(0, peers, weigh, zero)
    lax.fori_loop(0, peers, norm, zero)

    outs = []
    for c in range(chunks):

        @pl.loop(0, peers)
        def _(n):
            w = w_buf[n]
            for i in range(heads_chunk):
                h = c * heads_chunk + i
                wide_buf[n, :, i * HEAD_DIM:(i + 1) * HEAD_DIM] = jnp.broadcast_to(
                    w[:, h:h + 1], (rows, HEAD_DIM)
                )

        own_o[c].wait()
        drain(got_buf.at[c], o_recv.at[c])

        def visit(n, acc):
            mine = wide_buf[n] * got_buf[c, n].astype(jnp.float32)
            acc = jnp.where(fresh[n] == 1, mine, acc + mine)
            run_buf[n] = acc
            return acc

        lax.fori_loop(0, peers, visit, jnp.zeros((rows, wide), jnp.float32), unroll=2)
        picked = jnp.stack([run_buf[jnp.clip(ends[doc_ids[b]] - 1, 0, peers - 1)] for b in range(blocks)], axis=0)
        out_buf[c] = jnp.swapaxes(picked, 0, 1).astype(jnp.bfloat16)
        copy = pltpu.make_async_copy(
            out_buf.at[c], out_hbm.at[:, :, pl.ds(c * wide, wide)], out_sem.at[c]
        )
        copy.start()
        outs.append(copy)
    drain(s_buf, s_send)
    for c in range(q_chunks):
        drain(send_buf.at[c], q_send.at[c])
    for c in range(chunks):
        drain(o_buf.at[c], o_send.at[c])
        outs[c].wait()


def body(queries, kv_cache, page_counts, doc_ids):
    peers = lax.axis_size("ctx")
    rows, blocks, width = queries.shape
    assert kv_cache.shape[0] == 1 and width == 64 * HEAD_DIM
    wide = width // CHUNKS
    q_wide = width // Q_CHUNKS
    hbm_spec = pl.BlockSpec(memory_space=pltpu.HBM)
    smem_spec = pl.BlockSpec(memory_space=pltpu.SMEM)
    dma = pltpu.SemaphoreType.DMA
    q_pieces = pltpu.VMEM((Q_CHUNKS, peers, rows, q_wide), jnp.bfloat16)
    pieces = pltpu.VMEM((CHUNKS, peers, rows, wide), jnp.bfloat16)
    stats = pltpu.VMEM((peers, rows, 128), jnp.float32)
    return pl.pallas_call(
        functools.partial(attend_kernel, peers),
        out_shape=jax.ShapeDtypeStruct(queries.shape, jnp.bfloat16),
        in_specs=[smem_spec, smem_spec, hbm_spec, hbm_spec],
        out_specs=pl.BlockSpec(memory_space=pl.ANY),
        scratch_shapes=[
            pltpu.VMEM((Q_CHUNKS, rows, blocks, q_wide), jnp.bfloat16),
            pltpu.VMEM((Q_CHUNKS, blocks, rows, q_wide), jnp.bfloat16),
            q_pieces, q_pieces, pieces, pieces,
            stats, stats, stats, stats,
            pltpu.VMEM((peers, rows, wide), jnp.float32),
            pltpu.VMEM((peers, rows, wide), jnp.float32),
            pltpu.VMEM((CHUNKS, rows, blocks, wide), jnp.bfloat16),
            pltpu.VMEM(kv_cache.shape[1:], jnp.bfloat16),
            pltpu.SMEM((blocks,), jnp.int32),
            pltpu.SMEM((peers,), jnp.int32),
            pltpu.SMEM((peers,), jnp.int32),
            pltpu.SMEM((peers + 1,), jnp.int32),
            dma((Q_CHUNKS,)),
            dma((Q_CHUNKS,)), dma((Q_CHUNKS,)), dma((CHUNKS,)), dma((CHUNKS,)),
            dma(()), dma(()), dma((Q_CHUNKS,)), dma((CHUNKS,)), dma(()),
            dma(()), dma((CHUNKS,)),
        ],
        compiler_params=pltpu.CompilerParams(collective_id=0, has_side_effects=True),
    )(page_counts, doc_ids, queries, kv_cache)


def solution(mesh):
    placed = (
        P(("group", "ctx"), None, None),
        P(("group", "ctx"), None, None, None),
        P("group"),
        P("group"),
    )
    return jax.shard_map(
        body, mesh=mesh, in_specs=placed, out_specs=P(("group", "ctx"), None, None), check_vma=False
    )
```
